256 devices in a mesh: seq: 32 (over z, y_hi, core), ch: 8 (over y_lo, x).
Axes of the slice: x: 4, y: 4 (y_hi: 2, y_lo: 2; y = y_hi * 2 + y_lo), z: 8, core: 2. Of those that a mesh axis runs over, the one named last changes fastest.
Arguments:
- tokens: int32 [16384], P('seq'), may hold values from 0 to 4
- embedding: bfloat16 [5, 1024], P(None, 'ch'), may hold values from -4 to 4
- taps_dilated: float32 [3, 1024], P(None, 'ch'), may hold values from -3.5 to 3.5
- taps_short: float32 [3, 1024], P(None, 'ch'), may hold values from -3.5 to 3.5
- long_filter: float32 [16384, 1024], P('seq', 'ch'), may hold values from -1.5 to 1.5
- cotangent: bfloat16 [16384, 1024], P('seq', 'ch'), may hold values from -0.046875 to 0.046875
Outputs:
- mixed: bfloat16 [16384, 1024], P('seq', 'ch')
- filter_grad: float32 [16384, 1024], P('seq', 'ch')
The draws below stay inside these ranges and needn't reach their ends.
All inputs are finite; a program needn't handle non-finite values.
Results may differ from the reference program's by a relative error of at most 0.001.
Values may be sent and summed in bfloat16 or wider, within the bound.
A program may use at most 128 MiB of HBM per device.

```python
import math
import jax
import jax.numpy as jnp

D = 1024
NUCS = 5
TAPS = 3
SHORT_DILATION = 8
SEQUENCE_TOTAL = 16384


def draw_long_filter(key, part):
    decay_key, jitter_key, spike_key = jax.random.split(key, 3)
    delay_index = jnp.arange(SEQUENCE_TOTAL, dtype=jnp.float32)[:, None]
    log_rate = jax.random.uniform(decay_key, (1, D), jnp.float32, math.log(1.0 / (4.0 * SEQUENCE_TOTAL)), math.log(1.0 / 40.0))
    noise_part = jnp.clip(jax.random.normal(jitter_key, (SEQUENCE_TOTAL, D), jnp.float32), -6.0, 6.0)
    decay_rate = jnp.exp(log_rate)
    spike_position = jax.random.randint(spike_key, (4,), 1, SEQUENCE_TOTAL).astype(jnp.float32)
    spike_count = jnp.sum((delay_index >= spike_position[None, :]).astype(jnp.float32), axis=1, keepdims=True)
    multiplier = jnp.exp(spike_count * math.log(0.6))
    envelope = jnp.exp(-decay_rate * delay_index) * multiplier * jnp.sqrt(2.0 * decay_rate + 1.0 / SEQUENCE_TOTAL)
    return (noise_part * envelope).astype(jnp.float32)


def with_ends(entries, key, least, largest):
    longest = entries.shape.index(max(entries.shape))
    spots = []
    for shift in (0, 1):
        where = [jax.random.randint(jax.random.fold_in(key, axis), (), 0, length) for axis, length in enumerate(entries.shape)]
        where[longest] = (where[longest] + shift) % entries.shape[longest]
        spots.append(tuple(where))
    return entries.at[spots[0]].set(least).at[spots[1]].set(largest)


def shard_levels(stream_key, dims, shards, smallest, largest):
    gain = 1.0
    for dim, blocks in shards:
        draws = jax.random.uniform(jax.random.fold_in(jax.random.fold_in(stream_key, 6), dim), (blocks,), jnp.float32, smallest / len(shards), largest / len(shards))
        gain = gain * jnp.repeat(jnp.exp(draws), dims[dim] // blocks).reshape((-1,) + (1,) * (len(dims) - 1 - dim))
    return gain


def scatter_about(key, extent, scale, most, cuts=(), held_as=jnp.bfloat16):
    values = scale * jax.random.normal(key, extent, jnp.float32)
    if cuts:
        values = values * shard_levels(key, extent, cuts, -0.22, 0.18)
    return jnp.clip(values, -most, most).astype(held_as)


def setup_inputs(seed: int = 0) -> dict:
    streams_of = jax.random.split(jax.random.key(seed), 7)
    return {
        "tokens": with_ends(jax.random.randint(streams_of[0], (SEQUENCE_TOTAL,), 0, NUCS), jax.random.fold_in(streams_of[0], 1), 0, NUCS - 1).astype(jnp.int32),
        "embedding": scatter_about(streams_of[1], (NUCS, D), 1.0, 4.0, ((1, 8),)),
        "taps_dilated": scatter_about(streams_of[2], (TAPS, D), TAPS ** -0.5, 3.5, ((1, 8),), jnp.float32),
        "taps_short": scatter_about(streams_of[3], (TAPS, D), TAPS ** -0.5, 3.5, ((1, 8),), jnp.float32),
        "long_filter": draw_long_filter(jax.random.fold_in(streams_of[6], 71), 0),
        "cotangent": scatter_about(streams_of[5], (SEQUENCE_TOTAL, D), SEQUENCE_TOTAL ** -0.5, 0.046875, ((0, 32), (1, 8))),
    }


def reflect(values):
    return values[::-1, ::-1]


def short_convs(strand, taps_dilated, taps_short):
    source_rows = strand.astype(jnp.float32)
    inner = jnp.zeros((SEQUENCE_TOTAL, D), jnp.float32)
    for kernel_index in range(TAPS):
        shifted_rows = jnp.pad(source_rows, ((kernel_index * SHORT_DILATION, 0), (0, 0)))[:SEQUENCE_TOTAL]
        inner = inner + taps_dilated[kernel_index][None, :] * shifted_rows
    conv = jnp.zeros((SEQUENCE_TOTAL, D), jnp.float32)
    for kernel_index in range(TAPS):
        shifted_rows = jnp.pad(inner, ((kernel_index, 0), (0, 0)))[:SEQUENCE_TOTAL]
        conv = conv + taps_short[kernel_index][None, :] * shifted_rows
    return conv


def spectrum(values):
    return jnp.fft.rfft(values, n=2 * SEQUENCE_TOTAL, axis=0)


def back_wave(values):
    return jnp.fft.irfft(values, n=2 * SEQUENCE_TOTAL, axis=0)[:SEQUENCE_TOTAL].astype(jnp.float32)


def reference(tokens, embedding, taps_dilated, taps_short, long_filter, cotangent):
    hidden = jnp.take(embedding, tokens.astype(jnp.int32), axis=0)
    hidden_rc = reflect(hidden)
    cot_rc = reflect(cotangent)
    conv_f = short_convs(hidden, taps_dilated, taps_short)
    conv_rc = short_convs(hidden_rc, taps_dilated, taps_short)
    filter_spec = spectrum(long_filter)
    spec_f = spectrum(conv_f)
    spec_rc = spectrum(conv_rc)
    long_f = back_wave(filter_spec * spec_f)
    long_rc = back_wave(filter_spec * spec_rc)
    mixed = (hidden.astype(jnp.float32) * (long_f + reflect(long_rc))).astype(jnp.bfloat16)
    seed_f = cotangent.astype(jnp.float32) * hidden.astype(jnp.float32)
    seed_rc = cot_rc.astype(jnp.float32) * hidden_rc.astype(jnp.float32)
    filter_grad = back_wave(jnp.conj(spec_f) * spectrum(seed_f) + jnp.conj(spec_rc) * spectrum(seed_rc))
    return mixed, filter_grad
```

```python
import functools
import math

import jax
import jax.numpy as jnp
import numpy as np
from jax import lax
from jax.experimental import pallas as pl
from jax.experimental.pallas import tpu as pltpu
from jax.sharding import PartitionSpec as P

SHORT_DILATION = 8
LANES = 128
TILE = 8
MESH = pl.DeviceIdType.MESH


def split_table(table):
    high = table.astype(np.float32).astype(jnp.bfloat16)
    low = (table - high.astype(np.float64)).astype(np.float32).astype(jnp.bfloat16)
    return np.stack([high, low])


@functools.lru_cache(maxsize=None)
def dft_tables(seq_count, rows_per_block):
    rows = seq_count * rows_per_block
    total = rows * LANES
    k1 = np.arange(rows)
    angle = 2.0 * math.pi * ((np.arange(rows)[None, :] * (4 * k1[:, None] + 1)) % (4 * rows)) / (4 * rows)
    first = np.zeros((2, 2, rows, seq_count, 2, rows_per_block))
    for jj in range(2):
        first[jj, 0, :, :, jj, :] = np.cos(angle).reshape(rows, seq_count, rows_per_block)
        first[jj, 1, :, :, jj, :] = -np.sin(angle).reshape(rows, seq_count, rows_per_block)
    first = first.reshape(4 * rows, 2 * rows)
    n2 = np.arange(LANES)
    turn = 2.0 * math.pi * ((n2[None, :] * (4 * k1[:, None] + 1)) % (4 * total)) / (4 * total)
    twiddle = np.stack([np.cos(turn), -np.sin(turn)]).astype(np.float32)
    lane_angle = 2.0 * math.pi * ((n2[:, None] * n2[None, :]) % LANES) / LANES
    cos, sin = np.cos(lane_angle), np.sin(lane_angle)
    second = np.block([[cos, -sin], [sin, cos]])
    return (
        split_table(first),
        twiddle,
        split_table(second),
        split_table(second.T),
        split_table(first.T / total),
    )


class Place:
    def __init__(self, seq_count, ch_count):
        self.seq_count, self.ch_count = seq_count, ch_count
        self.members = 2 * seq_count
        self.s, self.c = lax.axis_index("seq"), lax.axis_index("ch")
        self.low = jnp.minimum(self.c, ch_count - 1 - self.c)
        self.side = jnp.where(2 * self.c >= ch_count, 1, 0)
        self.g = self.side * seq_count + self.s

    def peer(self, step):
        member = lax.rem(self.g + step, self.members)
        side = lax.div(member, self.seq_count)
        return member, side, lax.rem(member, self.seq_count)

    def device(self, side, s):
        return (s, self.low + side * (self.ch_count - 1 - 2 * self.low))

    def chunk_of(self, member, side):
        return member + side * (self.members - 1 - 2 * member)


def greet(place):
    barrier = pltpu.get_barrier_semaphore()

    def signal(step, carry):
        _, side, s = place.peer(step)
        pl.semaphore_signal(barrier, inc=1, device_id=place.device(side, s), device_id_type=MESH)
        return carry

    lax.fori_loop(1, place.members, signal, 0)
    return lambda: pl.semaphore_wait(barrier, place.members - 1)


def await_bytes(ref, sem):
    pltpu.make_async_copy(ref, ref, sem).wait()


def spread_kernel(seq_count, ch_count, tok_ref, par_ref, cot_ref, filt_ref, tok_all, par_all, cot_all, filt_all,
                  cot_send, filt_send, turned, send_sem, recv_sem):
    place = Place(seq_count, ch_count)
    await_all = greet(place)
    width = cot_ref.shape[1]
    parts = cot_ref.shape[0] // LANES
    chunks = cot_send.shape
    for r in range(parts):
        turned[pl.ds(r, width, stride=parts), :] = cot_ref[pl.ds(r * LANES, LANES), :].astype(jnp.float32).T
    cot_send[...] = turned[...].reshape(chunks).astype(jnp.bfloat16)
    for r in range(parts):
        filt_send[pl.ds(r, width, stride=parts), :] = filt_ref[pl.ds(r * LANES, LANES), :].T
    await_all()

    mirror = place.device(1 - place.side, place.s)
    params = pltpu.make_async_remote_copy(
        src_ref=par_ref, dst_ref=par_all.at[place.side], send_sem=send_sem.at[0], recv_sem=recv_sem.at[0],
        device_id=mirror, device_id_type=MESH)
    params.start()
    own_params = pltpu.make_async_copy(par_ref, par_all.at[place.side], send_sem.at[4])
    own_params.start()

    def send_tokens(step, carry):
        s = lax.rem(place.s + step, seq_count)
        pltpu.make_async_remote_copy(
            src_ref=tok_ref, dst_ref=tok_all.at[place.s], send_sem=send_sem.at[1], recv_sem=recv_sem.at[1],
            device_id=place.device(place.side, s), device_id_type=MESH).start()
        return carry

    lax.fori_loop(1, seq_count, send_tokens, 0)
    pltpu.make_async_copy(tok_ref, tok_all.at[place.s], recv_sem.at[1]).start()

    def rows_of(chunk):
        return pl.ds(pl.multiple_of(chunk * TILE, TILE), TILE)

    def send(step, carry):
        member, side, s = place.peer(step)
        chunk = place.chunk_of(member, place.side)
        device = place.device(side, s)
        pltpu.make_async_remote_copy(
            src_ref=filt_send.at[rows_of(chunk)], dst_ref=filt_all.at[rows_of(place.g)], send_sem=send_sem.at[3],
            recv_sem=recv_sem.at[3], device_id=device, device_id_type=MESH).start()
        pltpu.make_async_remote_copy(
            src_ref=cot_send.at[chunk], dst_ref=cot_all.at[place.g], send_sem=send_sem.at[2],
            recv_sem=recv_sem.at[2], device_id=device, device_id_type=MESH).start()
        return carry

    def send_pair(step, carry):
        send(step, carry)
        return send(place.members - step, carry)

    lax.fori_loop(1, seq_count, send_pair, 0)
    send(seq_count, 0)
    own = place.chunk_of(place.g, place.side)
    pltpu.make_async_copy(cot_send.at[own], cot_all.at[place.g], recv_sem.at[2]).start()
    pltpu.make_async_copy(filt_send.at[rows_of(own)], filt_all.at[rows_of(place.g)], recv_sem.at[3]).start()

    own_params.wait()
    params.wait()
    await_bytes(tok_all, recv_sem.at[1])
    await_bytes(cot_all, recv_sem.at[2])
    await_bytes(filt_all, recv_sem.at[3])
    await_bytes(tok_all.at[pl.ds(0, seq_count - 1)], send_sem.at[1])
    await_bytes(cot_send.at[pl.ds(0, place.members - 1)], send_sem.at[2])
    await_bytes(filt_send.at[pl.ds(0, TILE * (place.members - 1))], send_sem.at[3])


def split(x):
    high = x.astype(jnp.bfloat16)
    return high, (x - high.astype(jnp.float32)).astype(jnp.bfloat16)


def dot(a, b):
    return jnp.dot(a, b, preferred_element_type=jnp.float32)


def dot_left(table, x):
    high, low = split(x)
    return dot(table[0], high) + (dot(table[0], low) + dot(table[1], high))


def dot_right(x, table):
    high, low = split(x)
    return dot(high, table[0]) + (dot(high, table[1]) + dot(low, table[0]))


def shifted(x, amount, lane, row, parts):
    count = x.shape[0]
    zero = jnp.zeros_like(x[:1])
    if amount > 0:
        rolled = pltpu.roll(x, amount, axis=2)
        before = jnp.concatenate([zero, rolled[: count - 1]], axis=0)
        lower = jnp.where(row % parts == 0, pltpu.roll(before, parts + 1, axis=1), pltpu.roll(rolled, 1, axis=1))
        return jnp.where(lane >= amount, rolled, lower)
    rolled = pltpu.roll(x, LANES + amount, axis=2)
    after = jnp.concatenate([rolled[1:], zero], axis=0)
    upper = jnp.where(row % parts == parts - 1, pltpu.roll(after, parts - 1, axis=1), pltpu.roll(rolled, TILE - 1, axis=1))
    return jnp.where(lane < LANES + amount, rolled, upper)


def turn_kernel(seq_count, ch_count, kernel_count, nuc_count, tok_ref, par_ref, cot_ref, filt_ref, first_ref, twiddle_ref,
                second_ref, second_back_ref, first_back_ref, mixed_ref, grad_ref, hidden_ref, spec_ref):
    place = Place(seq_count, ch_count)
    rows = spec_ref.shape[1]
    parts = rows // seq_count
    flat = (seq_count * TILE, LANES)
    tiles = (seq_count, TILE, LANES)
    lane = lax.broadcasted_iota(jnp.int32, (1, TILE, LANES), 2)
    row = lax.broadcasted_iota(jnp.int32, (1, TILE, LANES), 1)
    width = par_ref.shape[2]
    par_lane = lax.broadcasted_iota(jnp.int32, (TILE, width), 1)
    par_row = lax.broadcasted_iota(jnp.int32, (TILE, width), 0)
    tokens = tok_ref[...]
    turn_re, turn_im = twiddle_ref[0], twiddle_ref[1]

    values = []
    for side in range(2):
        chunk = place.g if side == 0 else place.members - 1 - place.g
        here = par_lane == 2 * chunk + par_row // parts
        values.append([
            jnp.sum(jnp.where(here, par_ref[side, pl.ds(k, 1), :], 0.0), axis=1, keepdims=True)[None]
            for k in range(nuc_count + 2 * kernel_count)
        ])
    for side in range(2):
        hidden = jnp.zeros(tiles, jnp.float32)
        for letter in range(nuc_count):
            hidden = jnp.where(tokens == letter, values[side][letter], hidden)
        hidden_ref[side] = hidden

    def fir(side, tap_side, sign):
        taps = values[tap_side][nuc_count:]
        if tap_side != side:
            taps = [jnp.where(row < parts, t[:, TILE - 1:, :], t[:, :1, :]) for t in taps]
        source = hidden_ref[side]
        inner = taps[0] * source
        for k in range(1, kernel_count):
            inner = inner + taps[k] * shifted(source, sign * k * SHORT_DILATION, lane, row, parts)
        taps = taps[kernel_count:]
        conv = taps[0] * inner
        for k in range(1, kernel_count):
            conv = conv + taps[k] * shifted(inner, sign * k, lane, row, parts)
        return conv.reshape(flat)

    def transform(pair, slots):
        both = jnp.concatenate(pair, axis=1)
        section = dot_left(first_ref, both)
        stack = []
        for index in range(2):
            cols = slice(index * LANES, (index + 1) * LANES)
            for jj in range(2):
                re = section[2 * jj * rows:(2 * jj + 1) * rows, cols]
                im = section[(2 * jj + 1) * rows:(2 * jj + 2) * rows, cols]
                stack.append(jnp.concatenate([re * turn_re - im * turn_im, re * turn_im + im * turn_re], axis=1))
        spec = dot_right(jnp.concatenate(stack, axis=0), second_ref)
        for index in range(2):
            for jj in range(2):
                at = (index * 2 + jj) * rows
                spec_ref[slots[index] + jj] = spec[at:at + rows]

    for side in range(2):
        transform([fir(side, side, 1), fir(side, 1 - side, -1)], (8 * side, 8 * side + 2))
    for side in range(2):
        block = slice(side * seq_count, (side + 1) * seq_count)
        seed = cot_ref[block].astype(jnp.float32) * hidden_ref[side]
        filt = filt_ref[side * seq_count * TILE:(side + 1) * seq_count * TILE]
        transform([filt, seed.reshape(flat)], (8 * side + 4, 8 * side + 6))

    def parts_of(side, kind, jj):
        full = spec_ref[8 * side + 2 * kind + jj]
        return full[:, :LANES], full[:, LANES:]

    def times(a, b):
        return a[0] * b[0] - a[1] * b[1], a[0] * b[1] + a[1] * b[0]

    def times_conj(a, b):
        return a[0] * b[0] + a[1] * b[1], a[1] * b[0] - a[0] * b[1]

    for side in range(2):
        stack = []
        for jj in range(2):
            other = (1 - side, 1 - jj)
            u, v, h, s = [parts_of(side, kind, jj) for kind in range(4)]
            v_far, h_far, s_far = [parts_of(other[0], kind, other[1]) for kind in range(1, 4)]
            long_spec = [x + y for x, y in zip(times(h, u), times_conj(v, h_far))]
            grad_spec = [x + y for x, y in zip(times_conj(s, u), times_conj(v_far, s_far))]
            stack.append(jnp.concatenate(long_spec, axis=1))
            stack.append(jnp.concatenate(grad_spec, axis=1))
        section = dot_right(jnp.concatenate(stack, axis=0), second_back_ref)
        columns = []
        for index in range(2):
            pieces = []
            for jj in range(2):
                at = (2 * jj + index) * rows
                re, im = section[at:at + rows, :LANES], section[at:at + rows, LANES:]
                pieces.append(re * turn_re + im * turn_im)
                pieces.append(im * turn_re - re * turn_im)
            columns.append(jnp.concatenate(pieces, axis=0))
        wave = dot_left(first_back_ref, jnp.concatenate(columns, axis=1))
        block = slice(side * seq_count, (side + 1) * seq_count)
        mixed_ref[block] = (hidden_ref[side] * wave[:, :LANES].reshape(tiles)).astype(jnp.bfloat16)
        grad_ref[side * seq_count * TILE:(side + 1) * seq_count * TILE] = wave[:, LANES:]


def return_kernel(seq_count, ch_count, mixed_ref, grad_ref, mixed_all, grad_all, send_sem, recv_sem):
    place = Place(seq_count, ch_count)
    greet(place)()

    def rows_of(chunk):
        return pl.ds(pl.multiple_of(chunk * TILE, TILE), TILE)

    def send(step, carry):
        member, side, s = place.peer(step)
        chunk = place.chunk_of(place.g, side)
        device = place.device(side, s)
        pltpu.make_async_remote_copy(
            src_ref=grad_ref.at[rows_of(member)], dst_ref=grad_all.at[rows_of(chunk)], send_sem=send_sem.at[1],
            recv_sem=recv_sem.at[1], device_id=device, device_id_type=MESH).start()
        pltpu.make_async_remote_copy(
            src_ref=mixed_ref.at[member], dst_ref=mixed_all.at[chunk], send_sem=send_sem.at[0],
            recv_sem=recv_sem.at[0], device_id=device, device_id_type=MESH).start()
        return carry

    def send_pair(step, carry):
        send(step, carry)
        return send(place.members - step, carry)

    lax.fori_loop(1, seq_count, send_pair, 0)
    send(seq_count, 0)
    own = place.chunk_of(place.g, place.side)
    pltpu.make_async_copy(mixed_ref.at[place.g], mixed_all.at[own], recv_sem.at[0]).start()
    pltpu.make_async_copy(grad_ref.at[rows_of(place.g)], grad_all.at[rows_of(own)], recv_sem.at[1]).start()
    await_bytes(mixed_all, recv_sem.at[0])
    await_bytes(grad_all, recv_sem.at[1])
    await_bytes(mixed_ref.at[pl.ds(0, place.members - 1)], send_sem.at[0])
    await_bytes(grad_ref.at[pl.ds(0, TILE * (place.members - 1))], send_sem.at[1])


def settle_kernel(mixed_all, grad_all, mixed_ref, grad_ref, turned):
    parts = grad_ref.shape[0] // LANES
    width = grad_ref.shape[1]
    turned[...] = mixed_all[...].astype(jnp.float32).reshape(turned.shape)
    for r in range(parts):
        rows = pl.ds(r * LANES, LANES)
        mixed_ref[rows, :] = turned[pl.ds(r, width, stride=parts), :].T.astype(jnp.bfloat16)
        grad_ref[rows, :] = grad_all[pl.ds(r, width, stride=parts), :].T


def local(seq_count, ch_count, tokens, embedding, taps_dilated, taps_short, long_filter, cotangent):
    block_rows, width = cotangent.shape
    kernel_count = taps_dilated.shape[0]
    nuc_count = embedding.shape[0]
    parts = block_rows // LANES
    members = 2 * seq_count
    rows = parts * seq_count
    assert 2 * parts == TILE and width == 2 * members
    vmem = pl.BlockSpec(memory_space=pltpu.VMEM)
    f32, bf16 = jnp.float32, jnp.bfloat16
    shape = jax.ShapeDtypeStruct
    limit = 48 * 1024 * 1024

    own_tokens = tokens.reshape(parts, LANES)
    own_tokens = jnp.concatenate([own_tokens, own_tokens], axis=0)
    used = nuc_count + 2 * kernel_count
    params = jnp.concatenate(
        [embedding.astype(f32), taps_dilated, taps_short, jnp.zeros((-used % TILE, width), f32)], axis=0)

    tok_all, par_all, cot_all, filt_all = pl.pallas_call(
        functools.partial(spread_kernel, seq_count, ch_count),
        out_shape=(
            shape((seq_count, TILE, LANES), jnp.int32),
            shape((2,) + params.shape, f32),
            shape((members, TILE, LANES), bf16),
            shape((members * TILE, LANES), f32),
        ),
        in_specs=[vmem] * 4,
        out_specs=(vmem,) * 4,
        scratch_shapes=[
            pltpu.VMEM((members, TILE, LANES), bf16),
            pltpu.VMEM((members * TILE, LANES), f32),
            pltpu.VMEM((members * TILE, LANES), f32),
            pltpu.SemaphoreType.DMA((5,)),
            pltpu.SemaphoreType.DMA((4,)),
        ],
        compiler_params=pltpu.CompilerParams(collective_id=0, has_side_effects=True, vmem_limit_bytes=limit),
        name="spread",
    )(own_tokens, params, cotangent, long_filter)

    tables = [jnp.asarray(t) for t in dft_tables(seq_count, parts)]
    mixed, grad = pl.pallas_call(
        functools.partial(turn_kernel, seq_count, ch_count, kernel_count, nuc_count),
        out_shape=(shape((members, TILE, LANES), bf16), shape((members * TILE, LANES), f32)),
        in_specs=[vmem] * 9,
        out_specs=(vmem,) * 2,
        scratch_shapes=[
            pltpu.VMEM((2, seq_count, TILE, LANES), f32),
            pltpu.VMEM((16, rows, 2 * LANES), f32),
        ],
        compiler_params=pltpu.CompilerParams(vmem_limit_bytes=limit),
        name="turn",
    )(tok_all, par_all, cot_all, filt_all, *tables)

    mixed_all, grad_all = pl.pallas_call(
        functools.partial(return_kernel, seq_count, ch_count),
        out_shape=(shape((members, TILE, LANES), bf16), shape((members * TILE, LANES), f32)),
        in_specs=[vmem] * 2,
        out_specs=(vmem,) * 2,
        scratch_shapes=[pltpu.SemaphoreType.DMA((2,)), pltpu.SemaphoreType.DMA((2,))],
        compiler_params=pltpu.CompilerParams(collective_id=1, has_side_effects=True, vmem_limit_bytes=limit),
        name="return",
    )(mixed, grad)

    return pl.pallas_call(
        settle_kernel,
        out_shape=(shape((block_rows, width), bf16), shape((block_rows, width), f32)),
        in_specs=[vmem] * 2,
        out_specs=(vmem,) * 2,
        scratch_shapes=[pltpu.VMEM((members * TILE, LANES), f32)],
        name="settle",
    )(mixed_all, grad_all)


def solution(mesh):
    in_specs = (
        P("seq"),
        P(None, "ch"),
        P(None, "ch"),
        P(None, "ch"),
        P("seq", "ch"),
        P("seq", "ch"),
    )
    out_specs = (P("seq", "ch"), P("seq", "ch"))
    body = functools.partial(local, mesh.shape["seq"], mesh.shape["ch"])
    return jax.shard_map(body, mesh=mesh, in_specs=in_specs, out_specs=out_specs, check_vma=False)
```

```python
import functools
import math

import jax
import jax.numpy as jnp
import numpy as np
from jax import lax
from jax.experimental import pallas as pl
from jax.experimental.pallas import tpu as pltpu
from jax.sharding import PartitionSpec as P

SHORT_DILATION = 8
LANES = 128
TILE = 8
MESH = pl.DeviceIdType.MESH


def split_table(table):
    high = table.astype(np.float32).astype(jnp.bfloat16)
    low = (table - high.astype(np.float64)).astype(np.float32).astype(jnp.bfloat16)
    return np.stack([high, low])


@functools.lru_cache(maxsize=None)
def dft_tables(seq_count, rows_per_block):
    rows = seq_count * rows_per_block
    total = rows * LANES
    k1 = np.arange(rows)
    angle = 2.0 * math.pi * ((np.arange(rows)[None, :] * (4 * k1[:, None] + 1)) % (4 * rows)) / (4 * rows)
    first = np.zeros((2, 2, rows, seq_count, 2, rows_per_block))
    for jj in range(2):
        first[jj, 0, :, :, jj, :] = np.cos(angle).reshape(rows, seq_count, rows_per_block)
        first[jj, 1, :, :, jj, :] = -np.sin(angle).reshape(rows, seq_count, rows_per_block)
    first = first.reshape(4 * rows, 2 * rows)
    n2 = np.arange(LANES)
    turn = 2.0 * math.pi * ((n2[None, :] * (4 * k1[:, None] + 1)) % (4 * total)) / (4 * total)
    twiddle = np.stack([np.cos(turn), -np.sin(turn)]).astype(np.float32)
    lane_angle = 2.0 * math.pi * ((n2[:, None] * n2[None, :]) % LANES) / LANES
    cos, sin = np.cos(lane_angle), np.sin(lane_angle)
    second = np.block([[cos, -sin], [sin, cos]])
    return (
        split_table(first),
        twiddle,
        split_table(second),
        split_table(second.T),
        split_table(first.T / total),
    )


class Place:
    def __init__(self, seq_count, ch_count):
        self.seq_count, self.ch_count = seq_count, ch_count
        self.members = 2 * seq_count
        self.s, self.c = lax.axis_index("seq"), lax.axis_index("ch")
        self.low = jnp.minimum(self.c, ch_count - 1 - self.c)
        self.side = jnp.where(2 * self.c >= ch_count, 1, 0)
        self.g = self.side * seq_count + self.s

    def peer(self, step):
        member = self.g + step
        member = jnp.where(member >= self.members, member - self.members, member)
        side = jnp.where(member >= self.seq_count, 1, 0)
        return member, side, member - side * self.seq_count

    def near(self, step):
        s = self.s + step
        return jnp.where(s >= self.seq_count, s - self.seq_count, s)

    def device(self, side, s):
        return (s, self.low + side * (self.ch_count - 1 - 2 * self.low))

    def chunk_of(self, member, side):
        return member + side * (self.members - 1 - 2 * member)


def greet(place):
    barrier = pltpu.get_barrier_semaphore()

    def signal(step, carry):
        _, side, s = place.peer(step)
        pl.semaphore_signal(barrier, inc=1, device_id=place.device(side, s), device_id_type=MESH)
        return carry

    lax.fori_loop(1, place.members, signal, 0)
    return lambda: pl.semaphore_wait(barrier, place.members - 1)


def await_bytes(ref, sem):
    pltpu.make_async_copy(ref, ref, sem).wait()


def rows_of(chunk):
    return pl.ds(pl.multiple_of(chunk * TILE, TILE), TILE)


def split(x):
    high = x.astype(jnp.bfloat16)
    return high, (x - high.astype(jnp.float32)).astype(jnp.bfloat16)


def dot(a, b):
    return jnp.dot(a, b, preferred_element_type=jnp.float32)


def dot_left(table, x):
    high, low = split(x)
    return dot(table[0], high) + (dot(table[0], low) + dot(table[1], high))


def dot_right(x, table):
    high, low = split(x)
    return dot(high, table[0]) + (dot(high, table[1]) + dot(low, table[0]))


def shifted(x, amount, lane, row, parts):
    count = x.shape[0]
    zero = jnp.zeros_like(x[:1])
    if amount > 0:
        rolled = pltpu.roll(x, amount, axis=2)
        before = jnp.concatenate([zero, rolled[: count - 1]], axis=0)
        lower = jnp.where(row % parts == 0, pltpu.roll(before, parts + 1, axis=1), pltpu.roll(rolled, 1, axis=1))
        return jnp.where(lane >= amount, rolled, lower)
    rolled = pltpu.roll(x, LANES + amount, axis=2)
    after = jnp.concatenate([rolled[1:], zero], axis=0)
    upper = jnp.where(row % parts == parts - 1, pltpu.roll(after, parts - 1, axis=1), pltpu.roll(rolled, TILE - 1, axis=1))
    return jnp.where(lane < LANES + amount, rolled, upper)


def whole_kernel(seq_count, ch_count, tok_ref, emb_ref, dilated_ref, short_ref, cot_hbm, filt_hbm, first_hbm, twiddle_hbm,
                 second_hbm, second_back_hbm, first_back_hbm, mixed_all, grad_all,
                 cot_in, filt_in, turned, tok_send, par_send, cot_send, filt_send, tok_all, par_all, cot_all, filt_all,
                 first_ref, twiddle_ref, second_ref, second_back_ref, first_back_ref, hidden_ref, spec_ref,
                 mixed_ref, grad_ref, load_sem, table_sem, send_sem, recv_sem):
    place = Place(seq_count, ch_count)
    kernel_count, nuc_count = dilated_ref.shape[0], emb_ref.shape[0]
    width = cot_in.shape[1]
    parts = cot_in.shape[0] // LANES
    rows = parts * seq_count
    members = place.members

    load_filt = pltpu.make_async_copy(filt_hbm, filt_in, load_sem.at[0])
    load_cot = pltpu.make_async_copy(cot_hbm, cot_in, load_sem.at[1])
    load_filt.start()
    load_cot.start()
    await_all = greet(place)
    tables = [
        pltpu.make_async_copy(far, near, table_sem.at[index])
        for index, (far, near) in enumerate([
            (first_hbm, first_ref), (twiddle_hbm, twiddle_ref), (second_hbm, second_ref),
            (second_back_hbm, second_back_ref), (first_back_hbm, first_back_ref)])
    ]
    for table in tables:
        table.start()

    par_send[...] = jnp.zeros_like(par_send)
    par_send[pl.ds(0, nuc_count), :] = emb_ref[...].astype(jnp.float32)
    par_send[pl.ds(nuc_count, kernel_count), :] = dilated_ref[...]
    par_send[pl.ds(nuc_count + kernel_count, kernel_count), :] = short_ref[...]
    tok_send[...] = tok_ref[...].astype(jnp.float32).astype(jnp.bfloat16)
    load_filt.wait()
    for r in range(parts):
        filt_send[pl.ds(r, width, stride=parts), :] = filt_in[pl.ds(r * LANES, LANES), :].T
    load_cot.wait()
    for r in range(parts):
        turned[pl.ds(r, width, stride=parts), :] = cot_in[pl.ds(r * LANES, LANES), :].astype(jnp.float32).T
    cot_send[...] = turned[...].reshape(cot_send.shape).astype(jnp.bfloat16)
    await_all()

    params = pltpu.make_async_remote_copy(
        src_ref=par_send, dst_ref=par_all.at[place.side], send_sem=send_sem.at[0], recv_sem=recv_sem.at[0],
        device_id=place.device(1 - place.side, place.s), device_id_type=MESH)
    params.start()
    own_params = pltpu.make_async_copy(par_send, par_all.at[place.side], load_sem.at[2])
    own_params.start()

    def send_tokens(step, carry):
        pltpu.make_async_remote_copy(
            src_ref=tok_send, dst_ref=tok_all.at[place.s], send_sem=send_sem.at[1], recv_sem=recv_sem.at[1],
            device_id=place.device(place.side, place.near(step)), device_id_type=MESH).start()
        return carry

    lax.fori_loop(1, seq_count, send_tokens, 0)
    pltpu.make_async_copy(tok_send, tok_all.at[place.s], recv_sem.at[1]).start()

    def send(step, carry):
        member, side, s = place.peer(step)
        chunk = place.chunk_of(member, place.side)
        device = place.device(side, s)
        pltpu.make_async_remote_copy(
            src_ref=filt_send.at[rows_of(chunk)], dst_ref=filt_all.at[rows_of(place.g)], send_sem=send_sem.at[3],
            recv_sem=recv_sem.at[3], device_id=device, device_id_type=MESH).start()
        pltpu.make_async_remote_copy(
            src_ref=cot_send.at[chunk], dst_ref=cot_all.at[place.g], send_sem=send_sem.at[2],
            recv_sem=recv_sem.at[2], device_id=device, device_id_type=MESH).start()
        return carry

    def send_pair(step, carry):
        send(step, carry)
        return send(members - step, carry)

    lax.fori_loop(1, seq_count, send_pair, 0)
    send(seq_count, 0)
    own = place.chunk_of(place.g, place.side)
    pltpu.make_async_copy(cot_send.at[own], cot_all.at[place.g], recv_sem.at[2]).start()
    pltpu.make_async_copy(filt_send.at[rows_of(own)], filt_all.at[rows_of(place.g)], recv_sem.at[3]).start()

    for table in tables:
        table.wait()
    own_params.wait()
    params.wait()
    await_bytes(tok_all, recv_sem.at[1])

    flat = (seq_count * TILE, LANES)
    tiles = (seq_count, TILE, LANES)
    lane = lax.broadcasted_iota(jnp.int32, (1, TILE, LANES), 2)
    row = lax.broadcasted_iota(jnp.int32, (1, TILE, LANES), 1)
    width = par_all.shape[2]
    par_lane = lax.broadcasted_iota(jnp.int32, (TILE, width), 1)
    par_row = lax.broadcasted_iota(jnp.int32, (TILE, width), 0)
    tokens = tok_all[...].astype(jnp.float32)
    tokens = jnp.concatenate([tokens, tokens], axis=1)
    turn_re, turn_im = twiddle_ref[0], twiddle_ref[1]

    values = []
    for side in range(2):
        chunk = place.g if side == 0 else members - 1 - place.g
        here = par_lane == 2 * chunk + par_row // parts
        values.append([
            jnp.sum(jnp.where(here, par_all[side, pl.ds(k, 1), :], 0.0), axis=1, keepdims=True)[None]
            for k in range(nuc_count + 2 * kernel_count)
        ])
    for side in range(2):
        hidden = jnp.zeros(tiles, jnp.float32)
        for letter in range(nuc_count):
            hidden = jnp.where(tokens == float(letter), values[side][letter], hidden)
        hidden_ref[side] = hidden

    def fir(side, tap_side, sign):
        taps = values[tap_side][nuc_count:]
        if tap_side != side:
            taps = [jnp.where(row < parts, t[:, TILE - 1:, :], t[:, :1, :]) for t in taps]
        source = hidden_ref[side]
        inner = taps[0] * source
        for k in range(1, kernel_count):
            inner = inner + taps[k] * shifted(source, sign * k * SHORT_DILATION, lane, row, parts)
        taps = taps[kernel_count:]
        conv = taps[0] * inner
        for k in range(1, kernel_count):
            conv = conv + taps[k] * shifted(inner, sign * k, lane, row, parts)
        return conv.reshape(flat)

    def transform(pair, slots):
        both = jnp.concatenate(pair, axis=1)
        section = dot_left(first_ref, both)
        stack = []
        for index in range(2):
            cols = slice(index * LANES, (index + 1) * LANES)
            for jj in range(2):
                re = section[2 * jj * rows:(2 * jj + 1) * rows, cols]
                im = section[(2 * jj + 1) * rows:(2 * jj + 2) * rows, cols]
                stack.append(jnp.concatenate([re * turn_re - im * turn_im, re * turn_im + im * turn_re], axis=1))
        spec = dot_right(jnp.concatenate(stack, axis=0), second_ref)
        for index in range(2):
            for jj in range(2):
                at = (index * 2 + jj) * rows
                spec_ref[slots[index] + jj] = spec[at:at + rows]

    for side in range(2):
        transform([fir(side, side, 1), fir(side, 1 - side, -1)], (8 * side, 8 * side + 2))
    await_bytes(cot_all, recv_sem.at[2])
    await_bytes(filt_all, recv_sem.at[3])
    for side in range(2):
        block = slice(side * seq_count, (side + 1) * seq_count)
        seed = cot_all[block].astype(jnp.float32) * hidden_ref[side]
        filt = filt_all[side * seq_count * TILE:(side + 1) * seq_count * TILE]
        transform([filt, seed.reshape(flat)], (8 * side + 4, 8 * side + 6))

    def parts_of(side, kind, jj):
        full = spec_ref[8 * side + 2 * kind + jj]
        return full[:, :LANES], full[:, LANES:]

    def times(a, b):
        return a[0] * b[0] - a[1] * b[1], a[0] * b[1] + a[1] * b[0]

    def times_conj(a, b):
        return a[0] * b[0] + a[1] * b[1], a[1] * b[0] - a[0] * b[1]

    for side in range(2):
        stack = []
        for jj in range(2):
            other = (1 - side, 1 - jj)
            u, v, h, s = [parts_of(side, kind, jj) for kind in range(4)]
            v_far, h_far, s_far = [parts_of(other[0], kind, other[1]) for kind in range(1, 4)]
            long_spec = [x + y for x, y in zip(times(h, u), times_conj(v, h_far))]
            grad_spec = [x + y for x, y in zip(times_conj(s, u), times_conj(v_far, s_far))]
            stack.append(jnp.concatenate(long_spec, axis=1))
            stack.append(jnp.concatenate(grad_spec, axis=1))
        section = dot_right(jnp.concatenate(stack, axis=0), second_back_ref)
        columns = []
        for index in range(2):
            pieces = []
            for jj in range(2):
                at = (2 * jj + index) * rows
                re, im = section[at:at + rows, :LANES], section[at:at + rows, LANES:]
                pieces.append(re * turn_re + im * turn_im)
                pieces.append(im * turn_re - re * turn_im)
            columns.append(jnp.concatenate(pieces, axis=0))
        wave = dot_left(first_back_ref, jnp.concatenate(columns, axis=1))
        block = slice(side * seq_count, (side + 1) * seq_count)
        mixed_ref[block] = (hidden_ref[side] * wave[:, :LANES].reshape(tiles)).astype(jnp.bfloat16)
        grad_ref[side * seq_count * TILE:(side + 1) * seq_count * TILE] = wave[:, LANES:]

        def give_back(step, carry):
            s = place.near(step)
            device = place.device(side, s)
            member = side * seq_count + s
            chunk = place.chunk_of(place.g, side)
            pltpu.make_async_remote_copy(
                src_ref=grad_ref.at[rows_of(member)], dst_ref=grad_all.at[rows_of(chunk)], send_sem=send_sem.at[5],
                recv_sem=recv_sem.at[5], device_id=device, device_id_type=MESH).start()
            pltpu.make_async_remote_copy(
                src_ref=mixed_ref.at[member], dst_ref=mixed_all.at[chunk], send_sem=send_sem.at[4],
                recv_sem=recv_sem.at[4], device_id=device, device_id_type=MESH).start()
            return carry

        def give_pair(step, carry):
            give_back(step, carry)
            return give_back(seq_count - step, carry)

        lax.fori_loop(1, seq_count // 2, give_pair, 0)
        give_back(seq_count // 2, 0)

        @pl.when(place.side == side)
        def _():
            pltpu.make_async_copy(mixed_ref.at[place.g], mixed_all.at[own], recv_sem.at[4]).start()
            pltpu.make_async_copy(grad_ref.at[rows_of(place.g)], grad_all.at[rows_of(own)], recv_sem.at[5]).start()

        @pl.when(place.side != side)
        def _():
            give_back(0, 0)

    await_bytes(tok_all.at[pl.ds(0, seq_count - 1)], send_sem.at[1])
    await_bytes(cot_send.at[pl.ds(0, members - 1)], send_sem.at[2])
    await_bytes(filt_send.at[pl.ds(0, TILE * (members - 1))], send_sem.at[3])
    await_bytes(mixed_ref.at[pl.ds(0, members - 1)], send_sem.at[4])
    await_bytes(grad_ref.at[pl.ds(0, TILE * (members - 1))], send_sem.at[5])
    await_bytes(mixed_all, recv_sem.at[4])
    await_bytes(grad_all, recv_sem.at[5])


def settle_kernel(mixed_all, grad_all, mixed_ref, grad_ref, turned):
    parts = grad_ref.shape[0] // LANES
    width = grad_ref.shape[1]
    turned[...] = mixed_all[...].astype(jnp.float32).reshape(turned.shape)
    for r in range(parts):
        rows = pl.ds(r * LANES, LANES)
        mixed_ref[rows, :] = turned[pl.ds(r, width, stride=parts), :].T.astype(jnp.bfloat16)
        grad_ref[rows, :] = grad_all[pl.ds(r, width, stride=parts), :].T


def local(seq_count, ch_count, tokens, embedding, taps_dilated, taps_short, long_filter, cotangent):
    block_rows, width = cotangent.shape
    kernel_count = taps_dilated.shape[0]
    nuc_count = embedding.shape[0]
    parts = block_rows // LANES
    members = 2 * seq_count
    rows = parts * seq_count
    assert 2 * parts == TILE and width == 2 * members
    vmem = pl.BlockSpec(memory_space=pltpu.VMEM)
    f32, bf16 = jnp.float32, jnp.bfloat16
    shape = jax.ShapeDtypeStruct
    limit = 48 * 1024 * 1024

    any_space = pl.BlockSpec(memory_space=pl.ANY)
    tables = [jnp.asarray(t) for t in dft_tables(seq_count, parts)]
    mixed_all, grad_all = pl.pallas_call(
        functools.partial(whole_kernel, seq_count, ch_count),
        out_shape=(shape((members, TILE, LANES), bf16), shape((members * TILE, LANES), f32)),
        in_specs=[vmem] * 4 + [any_space] * 7,
        out_specs=(vmem,) * 2,
        scratch_shapes=[
            pltpu.VMEM((block_rows, width), bf16),
            pltpu.VMEM((block_rows, width), f32),
            pltpu.VMEM((members * TILE, LANES), f32),
            pltpu.VMEM((parts, LANES), bf16),
            pltpu.VMEM((-(-(nuc_count + 2 * kernel_count) // TILE) * TILE, width), f32),
            pltpu.VMEM((members, TILE, LANES), bf16),
            pltpu.VMEM((members * TILE, LANES), f32),
            pltpu.VMEM((seq_count, parts, LANES), bf16),
            pltpu.VMEM((2, -(-(nuc_count + 2 * kernel_count) // TILE) * TILE, width), f32),
            pltpu.VMEM((members, TILE, LANES), bf16),
            pltpu.VMEM((members * TILE, LANES), f32),
            *[pltpu.VMEM(t.shape, t.dtype) for t in tables],
            pltpu.VMEM((2, seq_count, TILE, LANES), f32),
            pltpu.VMEM((16, rows, 2 * LANES), f32),
            pltpu.VMEM((members, TILE, LANES), bf16),
            pltpu.VMEM((members * TILE, LANES), f32),
            pltpu.SemaphoreType.DMA((3,)),
            pltpu.SemaphoreType.DMA((5,)),
            pltpu.SemaphoreType.DMA((6,)),
            pltpu.SemaphoreType.DMA((6,)),
        ],
        compiler_params=pltpu.CompilerParams(collective_id=0, has_side_effects=True, vmem_limit_bytes=limit),
        name="whole",
    )(tokens.reshape(parts, LANES), embedding, taps_dilated, taps_short, cotangent, long_filter, *tables)

    return pl.pallas_call(
        settle_kernel,
        out_shape=(shape((block_rows, width), bf16), shape((block_rows, width), f32)),
        in_specs=[vmem] * 2,
        out_specs=(vmem,) * 2,
        scratch_shapes=[pltpu.VMEM((members * TILE, LANES), f32)],
        compiler_params=pltpu.CompilerParams(vmem_limit_bytes=8 * 1024 * 1024),
        name="settle",
    )(mixed_all, grad_all)


def solution(mesh):
    in_specs = (
        P("seq"),
        P(None, "ch"),
        P(None, "ch"),
        P(None, "ch"),
        P("seq", "ch"),
        P("seq", "ch"),
    )
    out_specs = (P("seq", "ch"), P("seq", "ch"))
    body = functools.partial(local, mesh.shape["seq"], mesh.shape["ch"])
    return jax.shard_map(body, mesh=mesh, in_specs=in_specs, out_specs=out_specs, check_vma=False)
```

```python
import functools
import math

import jax
import jax.numpy as jnp
import numpy as np
from jax import lax
from jax.experimental import pallas as pl
from jax.experimental.pallas import tpu as pltpu
from jax.sharding import PartitionSpec as P

SHORT_DILATION = 8
LANES = 128
TILE = 8
MESH = pl.DeviceIdType.MESH


def split_table(table):
    high = table.astype(np.float32).astype(jnp.bfloat16)
    low = (table - high.astype(np.float64)).astype(np.float32).astype(jnp.bfloat16)
    return np.stack([high, low])


@functools.lru_cache(maxsize=None)
def dft_tables(seq_count, rows_per_block):
    rows = seq_count * rows_per_block
    total = rows * LANES
    k1 = np.arange(rows)
    angle = 2.0 * math.pi * ((np.arange(rows)[None, :] * (4 * k1[:, None] + 1)) % (4 * rows)) / (4 * rows)
    first = np.zeros((2, 2, rows, seq_count, 2, rows_per_block))
    for jj in range(2):
        first[jj, 0, :, :, jj, :] = np.cos(angle).reshape(rows, seq_count, rows_per_block)
        first[jj, 1, :, :, jj, :] = -np.sin(angle).reshape(rows, seq_count, rows_per_block)
    first = first.reshape(4 * rows, 2 * rows)
    n2 = np.arange(LANES)
    turn = 2.0 * math.pi * ((n2[None, :] * (4 * k1[:, None] + 1)) % (4 * total)) / (4 * total)
    twiddle = np.stack([np.cos(turn), -np.sin(turn)]).astype(np.float32)
    lane_angle = 2.0 * math.pi * ((n2[:, None] * n2[None, :]) % LANES) / LANES
    cos, sin = np.cos(lane_angle), np.sin(lane_angle)
    second = np.block([[cos, -sin], [sin, cos]])
    return (
        split_table(first),
        twiddle,
        split_table(second),
        split_table(second.T),
        split_table(first.T / total),
    )


class Place:
    def __init__(self, seq_count, ch_count):
        self.seq_count, self.ch_count = seq_count, ch_count
        self.members = 2 * seq_count
        self.s, self.c = lax.axis_index("seq"), lax.axis_index("ch")
        self.low = jnp.minimum(self.c, ch_count - 1 - self.c)
        self.side = jnp.where(2 * self.c >= ch_count, 1, 0)
        self.g = self.side * seq_count + self.s

    def peer(self, step):
        member = self.g + step
        member = jnp.where(member >= self.members, member - self.members, member)
        side = jnp.where(member >= self.seq_count, 1, 0)
        return member, side, member - side * self.seq_count

    def near(self, step):
        s = self.s + step
        return jnp.where(s >= self.seq_count, s - self.seq_count, s)

    def device(self, side, s):
        return (s, self.low + side * (self.ch_count - 1 - 2 * self.low))

    def chunk_of(self, member, side):
        return member + side * (self.members - 1 - 2 * member)


def greet(place):
    barrier = pltpu.get_barrier_semaphore()

    def signal(step, carry):
        _, side, s = place.peer(step)
        pl.semaphore_signal(barrier, inc=1, device_id=place.device(side, s), device_id_type=MESH)
        return carry

    lax.fori_loop(1, place.members, signal, 0)
    return lambda: pl.semaphore_wait(barrier, place.members - 1)


def await_bytes(ref, sem):
    pltpu.make_async_copy(ref, ref, sem).wait()


def rows_of(chunk):
    return pl.ds(pl.multiple_of(chunk * TILE, TILE), TILE)


def split(x):
    high = x.astype(jnp.bfloat16)
    return high, (x - high.astype(jnp.float32)).astype(jnp.bfloat16)


def dot(a, b):
    return jnp.dot(a, b, preferred_element_type=jnp.float32)


def dot_left(table, x):
    high, low = split(x)
    return dot(table[0], high) + (dot(table[0], low) + dot(table[1], high))


def dot_right(x, table):
    high, low = split(x)
    return dot(high, table[0]) + (dot(high, table[1]) + dot(low, table[0]))


def shifted(x, amount, lane, row, parts):
    count = x.shape[0]
    zero = jnp.zeros_like(x[:1])
    if amount > 0:
        rolled = pltpu.roll(x, amount, axis=2)
        before = jnp.concatenate([zero, rolled[: count - 1]], axis=0)
        lower = jnp.where(row % parts == 0, pltpu.roll(before, parts + 1, axis=1), pltpu.roll(rolled, 1, axis=1))
        return jnp.where(lane >= amount, rolled, lower)
    rolled = pltpu.roll(x, LANES + amount, axis=2)
    after = jnp.concatenate([rolled[1:], zero], axis=0)
    upper = jnp.where(row % parts == parts - 1, pltpu.roll(after, parts - 1, axis=1), pltpu.roll(rolled, TILE - 1, axis=1))
    return jnp.where(lane < LANES + amount, rolled, upper)


def whole_kernel(seq_count, ch_count, tok_hbm, emb_hbm, dilated_hbm, short_hbm, cot_hbm, filt_hbm, first_hbm, twiddle_hbm,
                 second_hbm, second_back_hbm, first_back_hbm, mixed_all, grad_all,
                 tok_ref, emb_ref, dilated_ref, short_ref, cot_in, filt_in, turned, tok_send, par_send, cot_send, filt_send, tok_all, par_all, cot_all, filt_all,
                 first_ref, twiddle_ref, second_ref, second_back_ref, first_back_ref, hidden_ref, spec_ref,
                 mixed_ref, grad_ref, small_sem, load_sem, table_sem, send_sem, recv_sem):
    place = Place(seq_count, ch_count)
    kernel_count, nuc_count = dilated_ref.shape[0], emb_ref.shape[0]
    width = cot_in.shape[1]
    parts = cot_in.shape[0] // LANES
    rows = parts * seq_count
    members = place.members

    load_filt = pltpu.make_async_copy(filt_hbm, filt_in, load_sem.at[0])
    load_cot = pltpu.make_async_copy(cot_hbm, cot_in, load_sem.at[1])
    load_filt.start()
    load_cot.start()
    small = [
        pltpu.make_async_copy(far, near, small_sem.at[index])
        for index, (far, near) in enumerate([
            (tok_hbm, tok_ref), (emb_hbm, emb_ref), (dilated_hbm, dilated_ref), (short_hbm, short_ref)])
    ]
    for load in small:
        load.start()
    await_all = greet(place)
    tables = [
        pltpu.make_async_copy(far, near, table_sem.at[index])
        for index, (far, near) in enumerate([
            (first_hbm, first_ref), (twiddle_hbm, twiddle_ref), (second_hbm, second_ref),
            (second_back_hbm, second_back_ref), (first_back_hbm, first_back_ref)])
    ]
    for table in tables:
        table.start()

    for load in small:
        load.wait()
    par_send[...] = jnp.zeros_like(par_send)
    par_send[pl.ds(0, nuc_count), :] = emb_ref[...].astype(jnp.float32)
    par_send[pl.ds(nuc_count, kernel_count), :] = dilated_ref[...]
    par_send[pl.ds(nuc_count + kernel_count, kernel_count), :] = short_ref[...]
    tok_send[...] = tok_ref[...].astype(jnp.float32).astype(jnp.bfloat16)
    load_filt.wait()
    for r in range(parts):
        filt_send[pl.ds(r, width, stride=parts), :] = filt_in[pl.ds(r * LANES, LANES), :].T
    load_cot.wait()
    for r in range(parts):
        turned[pl.ds(r, width, stride=parts), :] = cot_in[pl.ds(r * LANES, LANES), :].astype(jnp.float32).T
    cot_send[...] = turned[...].reshape(cot_send.shape).astype(jnp.bfloat16)
    await_all()

    params = pltpu.make_async_remote_copy(
        src_ref=par_send, dst_ref=par_all.at[place.side], send_sem=send_sem.at[0], recv_sem=recv_sem.at[0],
        device_id=place.device(1 - place.side, place.s), device_id_type=MESH)
    params.start()
    own_params = pltpu.make_async_copy(par_send, par_all.at[place.side], load_sem.at[2])
    own_params.start()

    def send_tokens(step, carry):
        pltpu.make_async_remote_copy(
            src_ref=tok_send, dst_ref=tok_all.at[place.s], send_sem=send_sem.at[1], recv_sem=recv_sem.at[1],
            device_id=place.device(place.side, place.near(step)), device_id_type=MESH).start()
        return carry

    lax.fori_loop(1, seq_count, send_tokens, 0)
    pltpu.make_async_copy(tok_send, tok_all.at[place.s], recv_sem.at[1]).start()

    def send(step, carry):
        member, side, s = place.peer(step)
        chunk = place.chunk_of(member, place.side)
        device = place.device(side, s)
        pltpu.make_async_remote_copy(
            src_ref=filt_send.at[rows_of(chunk)], dst_ref=filt_all.at[rows_of(place.g)], send_sem=send_sem.at[3],
            recv_sem=recv_sem.at[3], device_id=device, device_id_type=MESH).start()
        pltpu.make_async_remote_copy(
            src_ref=cot_send.at[chunk], dst_ref=cot_all.at[place.g], send_sem=send_sem.at[2],
            recv_sem=recv_sem.at[2], device_id=device, device_id_type=MESH).start()
        return carry

    def send_pair(step, carry):
        send(step, carry)
        return send(members - step, carry)

    lax.fori_loop(1, seq_count, send_pair, 0)
    send(seq_count, 0)
    own = place.chunk_of(place.g, place.side)
    pltpu.make_async_copy(cot_send.at[own], cot_all.at[place.g], recv_sem.at[2]).start()
    pltpu.make_async_copy(filt_send.at[rows_of(own)], filt_all.at[rows_of(place.g)], recv_sem.at[3]).start()

    for table in tables:
        table.wait()
    own_params.wait()
    params.wait()
    await_bytes(tok_all, recv_sem.at[1])

    flat = (seq_count * TILE, LANES)
    tiles = (seq_count, TILE, LANES)
    lane = lax.broadcasted_iota(jnp.int32, (1, TILE, LANES), 2)
    row = lax.broadcasted_iota(jnp.int32, (1, TILE, LANES), 1)
    width = par_all.shape[2]
    par_lane = lax.broadcasted_iota(jnp.int32, (TILE, width), 1)
    par_row = lax.broadcasted_iota(jnp.int32, (TILE, width), 0)
    tokens = tok_all[...].astype(jnp.float32)
    tokens = jnp.concatenate([tokens, tokens], axis=1)
    turn_re, turn_im = twiddle_ref[0], twiddle_ref[1]

    values = []
    for side in range(2):
        chunk = place.g if side == 0 else members - 1 - place.g
        here = par_lane == 2 * chunk + par_row // parts
        values.append([
            jnp.sum(jnp.where(here, par_all[side, pl.ds(k, 1), :], 0.0), axis=1, keepdims=True)[None]
            for k in range(nuc_count + 2 * kernel_count)
        ])
    for side in range(2):
        hidden = jnp.zeros(tiles, jnp.float32)
        for letter in range(nuc_count):
            hidden = jnp.where(tokens == float(letter), values[side][letter], hidden)
        hidden_ref[side] = hidden

    def fir(side, tap_side, sign):
        taps = values[tap_side][nuc_count:]
        if tap_side != side:
            taps = [jnp.where(row < parts, t[:, TILE - 1:, :], t[:, :1, :]) for t in taps]
        source = hidden_ref[side]
        inner = taps[0] * source
        for k in range(1, kernel_count):
            inner = inner + taps[k] * shifted(source, sign * k * SHORT_DILATION, lane, row, parts)
        taps = taps[kernel_count:]
        conv = taps[0] * inner
        for k in range(1, kernel_count):
            conv = conv + taps[k] * shifted(inner, sign * k, lane, row, parts)
        return conv.reshape(flat)

    def transform(pair, slots):
        both = jnp.concatenate(pair, axis=1)
        section = dot_left(first_ref, both)
        stack = []
        for index in range(2):
            cols = slice(index * LANES, (index + 1) * LANES)
            for jj in range(2):
                re = section[2 * jj * rows:(2 * jj + 1) * rows, cols]
                im = section[(2 * jj + 1) * rows:(2 * jj + 2) * rows, cols]
                stack.append(jnp.concatenate([re * turn_re - im * turn_im, re * turn_im + im * turn_re], axis=1))
        spec = dot_right(jnp.concatenate(stack, axis=0), second_ref)
        for index in range(2):
            for jj in range(2):
                at = (index * 2 + jj) * rows
                spec_ref[slots[index] + jj] = spec[at:at + rows]

    for side in range(2):
        transform([fir(side, side, 1), fir(side, 1 - side, -1)], (8 * side, 8 * side + 2))
    await_bytes(cot_all, recv_sem.at[2])
    await_bytes(filt_all, recv_sem.at[3])
    for side in range(2):
        block = slice(side * seq_count, (side + 1) * seq_count)
        seed = cot_all[block].astype(jnp.float32) * hidden_ref[side]
        filt = filt_all[side * seq_count * TILE:(side + 1) * seq_count * TILE]
        transform([filt, seed.reshape(flat)], (8 * side + 4, 8 * side + 6))

    def parts_of(side, kind, jj):
        full = spec_ref[8 * side + 2 * kind + jj]
        return full[:, :LANES], full[:, LANES:]

    def times(a, b):
        return a[0] * b[0] - a[1] * b[1], a[0] * b[1] + a[1] * b[0]

    def times_conj(a, b):
        return a[0] * b[0] + a[1] * b[1], a[1] * b[0] - a[0] * b[1]

    for side in range(2):
        stack = []
        for jj in range(2):
            other = (1 - side, 1 - jj)
            u, v, h, s = [parts_of(side, kind, jj) for kind in range(4)]
            v_far, h_far, s_far = [parts_of(other[0], kind, other[1]) for kind in range(1, 4)]
            long_spec = [x + y for x, y in zip(times(h, u), times_conj(v, h_far))]
            grad_spec = [x + y for x, y in zip(times_conj(s, u), times_conj(v_far, s_far))]
            stack.append(jnp.concatenate(long_spec, axis=1))
            stack.append(jnp.concatenate(grad_spec, axis=1))
        section = dot_right(jnp.concatenate(stack, axis=0), second_back_ref)
        columns = []
        for index in range(2):
            pieces = []
            for jj in range(2):
                at = (2 * jj + index) * rows
                re, im = section[at:at + rows, :LANES], section[at:at + rows, LANES:]
                pieces.append(re * turn_re + im * turn_im)
                pieces.append(im * turn_re - re * turn_im)
            columns.append(jnp.concatenate(pieces, axis=0))
        wave = dot_left(first_back_ref, jnp.concatenate(columns, axis=1))
        block = slice(side * seq_count, (side + 1) * seq_count)
        mixed_ref[block] = (hidden_ref[side] * wave[:, :LANES].reshape(tiles)).astype(jnp.bfloat16)
        grad_ref[side * seq_count * TILE:(side + 1) * seq_count * TILE] = wave[:, LANES:]

        def give_back(step, carry):
            s = place.near(step)
            device = place.device(side, s)
            member = side * seq_count + s
            chunk = place.chunk_of(place.g, side)
            pltpu.make_async_remote_copy(
                src_ref=grad_ref.at[rows_of(member)], dst_ref=grad_all.at[rows_of(chunk)], send_sem=send_sem.at[5],
                recv_sem=recv_sem.at[5], device_id=device, device_id_type=MESH).start()
            pltpu.make_async_remote_copy(
                src_ref=mixed_ref.at[member], dst_ref=mixed_all.at[chunk], send_sem=send_sem.at[4],
                recv_sem=recv_sem.at[4], device_id=device, device_id_type=MESH).start()
            return carry

        def give_pair(step, carry):
            give_back(step, carry)
            return give_back(seq_count - step, carry)

        lax.fori_loop(1, seq_count // 2, give_pair, 0)
        give_back(seq_count // 2, 0)

        @pl.when(place.side == side)
        def _():
            pltpu.make_async_copy(mixed_ref.at[place.g], mixed_all.at[own], recv_sem.at[4]).start()
            pltpu.make_async_copy(grad_ref.at[rows_of(place.g)], grad_all.at[rows_of(own)], recv_sem.at[5]).start()

        @pl.when(place.side != side)
        def _():
            give_back(0, 0)

    await_bytes(tok_all.at[pl.ds(0, seq_count - 1)], send_sem.at[1])
    await_bytes(cot_send.at[pl.ds(0, members - 1)], send_sem.at[2])
    await_bytes(filt_send.at[pl.ds(0, TILE * (members - 1))], send_sem.at[3])
    await_bytes(mixed_ref.at[pl.ds(0, members - 1)], send_sem.at[4])
    await_bytes(grad_ref.at[pl.ds(0, TILE * (members - 1))], send_sem.at[5])
    await_bytes(mixed_all, recv_sem.at[4])
    await_bytes(grad_all, recv_sem.at[5])


def settle_kernel(mixed_hbm, grad_hbm, mixed_ref, grad_ref, mixed_all, grad_all, turned, sem):
    parts = grad_ref.shape[0] // LANES
    width = grad_ref.shape[1]
    load_mixed = pltpu.make_async_copy(mixed_hbm, mixed_all, sem.at[0])
    load_grad = pltpu.make_async_copy(grad_hbm, grad_all, sem.at[1])
    load_mixed.start()
    load_grad.start()
    load_mixed.wait()
    turned[...] = mixed_all[...].astype(jnp.float32).reshape(turned.shape)
    for r in range(parts):
        mixed_ref[pl.ds(r * LANES, LANES), :] = turned[pl.ds(r, width, stride=parts), :].T.astype(jnp.bfloat16)
    load_grad.wait()
    for r in range(parts):
        grad_ref[pl.ds(r * LANES, LANES), :] = grad_all[pl.ds(r, width, stride=parts), :].T


def local(seq_count, ch_count, tokens, embedding, taps_dilated, taps_short, long_filter, cotangent):
    block_rows, width = cotangent.shape
    kernel_count = taps_dilated.shape[0]
    nuc_count = embedding.shape[0]
    parts = block_rows // LANES
    members = 2 * seq_count
    rows = parts * seq_count
    assert 2 * parts == TILE and width == 2 * members
    vmem = pl.BlockSpec(memory_space=pltpu.VMEM)
    f32, bf16 = jnp.float32, jnp.bfloat16
    shape = jax.ShapeDtypeStruct
    limit = 67043328

    far = pl.BlockSpec(memory_space=pltpu.HBM)
    tables = [jnp.asarray(t) for t in dft_tables(seq_count, parts)]
    mixed_all, grad_all = pl.pallas_call(
        functools.partial(whole_kernel, seq_count, ch_count),
        out_shape=(shape((members, TILE, LANES), bf16), shape((members * TILE, LANES), f32)),
        in_specs=[far] * 11,
        out_specs=(far,) * 2,
        scratch_shapes=[
            pltpu.VMEM((parts, LANES), jnp.int32),
            pltpu.VMEM(embedding.shape, bf16),
            pltpu.VMEM(taps_dilated.shape, f32),
            pltpu.VMEM(taps_short.shape, f32),
            pltpu.VMEM((block_rows, width), bf16),
            pltpu.VMEM((block_rows, width), f32),
            pltpu.VMEM((members * TILE, LANES), f32),
            pltpu.VMEM((parts, LANES), bf16),
            pltpu.VMEM((-(-(nuc_count + 2 * kernel_count) // TILE) * TILE, width), f32),
            pltpu.VMEM((members, TILE, LANES), bf16),
            pltpu.VMEM((members * TILE, LANES), f32),
            pltpu.VMEM((seq_count, parts, LANES), bf16),
            pltpu.VMEM((2, -(-(nuc_count + 2 * kernel_count) // TILE) * TILE, width), f32),
            pltpu.VMEM((members, TILE, LANES), bf16),
            pltpu.VMEM((members * TILE, LANES), f32),
            *[pltpu.VMEM(t.shape, t.dtype) for t in tables],
            pltpu.VMEM((2, seq_count, TILE, LANES), f32),
            pltpu.VMEM((16, rows, 2 * LANES), f32),
            pltpu.VMEM((members, TILE, LANES), bf16),
            pltpu.VMEM((members * TILE, LANES), f32),
            pltpu.SemaphoreType.DMA((4,)),
            pltpu.SemaphoreType.DMA((3,)),
            pltpu.SemaphoreType.DMA((5,)),
            pltpu.SemaphoreType.DMA((6,)),
            pltpu.SemaphoreType.DMA((6,)),
        ],
        compiler_params=pltpu.CompilerParams(collective_id=0, has_side_effects=True, vmem_limit_bytes=limit),
        name="whole",
    )(tokens.reshape(parts, LANES), embedding, taps_dilated, taps_short, cotangent, long_filter, *tables)

    return pl.pallas_call(
        settle_kernel,
        out_shape=(shape((block_rows, width), bf16), shape((block_rows, width), f32)),
        in_specs=[far] * 2,
        out_specs=(vmem,) * 2,
        scratch_shapes=[
            pltpu.VMEM((members, TILE, LANES), bf16),
            pltpu.VMEM((members * TILE, LANES), f32),
            pltpu.VMEM((members * TILE, LANES), f32),
            pltpu.SemaphoreType.DMA((2,)),
        ],
        compiler_params=pltpu.CompilerParams(vmem_limit_bytes=limit),
        name="settle",
    )(mixed_all, grad_all)


def solution(mesh):
    in_specs = (
        P("seq"),
        P(None, "ch"),
        P(None, "ch"),
        P(None, "ch"),
        P("seq", "ch"),
        P("seq", "ch"),
    )
    out_specs = (P("seq", "ch"), P("seq", "ch"))
    body = functools.partial(local, mesh.shape["seq"], mesh.shape["ch"])
    return jax.shard_map(body, mesh=mesh, in_specs=in_specs, out_specs=out_specs, check_vma=False)
```

```python
import functools
import math

import jax
import jax.numpy as jnp
import numpy as np
from jax import lax
from jax.experimental import pallas as pl
from jax.experimental.pallas import tpu as pltpu
from jax.sharding import PartitionSpec as P

SHORT_DILATION = 8
LANES = 128
TILE = 8
MESH = pl.DeviceIdType.MESH
COUNTS = 32700.0
LEAST = 1e-33


def split_table(table):
    high = table.astype(np.float32).astype(jnp.bfloat16)
    low = (table - high.astype(np.float64)).astype(np.float32).astype(jnp.bfloat16)
    return np.stack([high, low])


@functools.lru_cache(maxsize=None)
def dft_tables(seq_count, rows_per_block):
    rows = seq_count * rows_per_block
    total = rows * LANES
    k1 = np.arange(rows)
    angle = 2.0 * math.pi * ((np.arange(rows)[None, :] * (4 * k1[:, None] + 1)) % (4 * rows)) / (4 * rows)
    first = np.zeros((2, 2, rows, seq_count, 2, rows_per_block))
    for jj in range(2):
        first[jj, 0, :, :, jj, :] = np.cos(angle).reshape(rows, seq_count, rows_per_block)
        first[jj, 1, :, :, jj, :] = -np.sin(angle).reshape(rows, seq_count, rows_per_block)
    first = first.reshape(4 * rows, 2 * rows)
    n2 = np.arange(LANES)
    turn = 2.0 * math.pi * ((n2[None, :] * (4 * k1[:, None] + 1)) % (4 * total)) / (4 * total)
    twiddle = np.stack([np.cos(turn), -np.sin(turn)]).astype(np.float32)
    lane_angle = 2.0 * math.pi * ((n2[:, None] * n2[None, :]) % LANES) / LANES
    cos, sin = np.cos(lane_angle), np.sin(lane_angle)
    second = np.block([[cos, -sin], [sin, cos]])
    return (
        split_table(first),
        twiddle,
        split_table(second),
        split_table(second.T),
        split_table(first.T / total),
    )


class Place:
    def __init__(self, seq_count, ch_count):
        self.seq_count, self.ch_count = seq_count, ch_count
        self.members = 2 * seq_count
        self.s, self.c = lax.axis_index("seq"), lax.axis_index("ch")
        self.low = jnp.minimum(self.c, ch_count - 1 - self.c)
        self.side = jnp.where(2 * self.c >= ch_count, 1, 0)
        self.g = self.side * seq_count + self.s

    def peer(self, step):
        member = self.g + step
        member = jnp.where(member >= self.members, member - self.members, member)
        side = jnp.where(member >= self.seq_count, 1, 0)
        return member, side, member - side * self.seq_count

    def near(self, step):
        s = self.s + step
        return jnp.where(s >= self.seq_count, s - self.seq_count, s)

    def device(self, side, s):
        return (s, self.low + side * (self.ch_count - 1 - 2 * self.low))

    def chunk_of(self, member, side):
        return member + side * (self.members - 1 - 2 * member)


def greet(place):
    barrier = pltpu.get_barrier_semaphore()

    def signal(step, carry):
        _, side, s = place.peer(step)
        pl.semaphore_signal(barrier, inc=1, device_id=place.device(side, s), device_id_type=MESH)
        return carry

    lax.fori_loop(1, place.members, signal, 0)
    return lambda: pl.semaphore_wait(barrier, place.members - 1)


def await_bytes(ref, sem):
    pltpu.make_async_copy(ref, ref, sem).wait()


def steps_for(largest):
    return COUNTS / largest


def fixed_point(x):
    return jnp.floor(x + 0.5).astype(jnp.int32).astype(jnp.int16)


def floating(x):
    return x.astype(jnp.int32).astype(jnp.float32)


def split(x):
    high = x.astype(jnp.bfloat16)
    return high, (x - high.astype(jnp.float32)).astype(jnp.bfloat16)


def dot(a, b):
    return jnp.dot(a, b, preferred_element_type=jnp.float32)


def dot_left(table, x):
    high, low = split(x)
    return dot(table[0], high) + (dot(table[0], low) + dot(table[1], high))


def dot_right(x, table):
    high, low = split(x)
    return dot(high, table[0]) + (dot(high, table[1]) + dot(low, table[0]))


def shifted(x, amount, lane, row, parts):
    count = x.shape[0]
    zero = jnp.zeros_like(x[:1])
    if amount > 0:
        rolled = pltpu.roll(x, amount, axis=2)
        before = jnp.concatenate([zero, rolled[: count - 1]], axis=0)
        lower = jnp.where(row % parts == 0, pltpu.roll(before, parts + 1, axis=1), pltpu.roll(rolled, 1, axis=1))
        return jnp.where(lane >= amount, rolled, lower)
    rolled = pltpu.roll(x, LANES + amount, axis=2)
    after = jnp.concatenate([rolled[1:], zero], axis=0)
    upper = jnp.where(row % parts == parts - 1, pltpu.roll(after, parts - 1, axis=1), pltpu.roll(rolled, TILE - 1, axis=1))
    return jnp.where(lane < LANES + amount, rolled, upper)


def whole_kernel(seq_count, ch_count, tok_hbm, emb_hbm, dilated_hbm, short_hbm, cot_hbm, filt_hbm, first_hbm, twiddle_hbm,
                 second_hbm, second_back_hbm, first_back_hbm, mixed_all, grad_all, grad_size_all,
                 tok_ref, emb_ref, dilated_ref, short_ref, cot_in, filt_in, turned, tok_send, par_send, cot_send, filt_send, filt_size, tok_all, par_all, cot_all, filt_all, filt_size_all,
                 first_ref, twiddle_ref, second_ref, second_back_ref, first_back_ref, hidden_ref, spec_ref,
                 mixed_ref, grad_ref, grad_size, small_sem, load_sem, table_sem, send_sem, recv_sem):
    place = Place(seq_count, ch_count)
    kernel_count, nuc_count = dilated_ref.shape[0], emb_ref.shape[0]
    width = cot_in.shape[1]
    parts = cot_in.shape[0] // LANES
    rows = parts * seq_count
    members = place.members

    load_filt = pltpu.make_async_copy(filt_hbm, filt_in, load_sem.at[0])
    load_cot = pltpu.make_async_copy(cot_hbm, cot_in, load_sem.at[1])
    load_filt.start()
    load_cot.start()
    small = [
        pltpu.make_async_copy(far, near, small_sem.at[index])
        for index, (far, near) in enumerate([
            (tok_hbm, tok_ref), (emb_hbm, emb_ref), (dilated_hbm, dilated_ref), (short_hbm, short_ref)])
    ]
    for load in small:
        load.start()
    await_all = greet(place)
    tables = [
        pltpu.make_async_copy(far, near, table_sem.at[index])
        for index, (far, near) in enumerate([
            (first_hbm, first_ref), (twiddle_hbm, twiddle_ref), (second_hbm, second_ref),
            (second_back_hbm, second_back_ref), (first_back_hbm, first_back_ref)])
    ]
    for table in tables:
        table.start()

    for load in small:
        load.wait()
    par_send[...] = jnp.zeros_like(par_send)
    par_send[pl.ds(0, nuc_count), :] = emb_ref[...].astype(jnp.float32)
    par_send[pl.ds(nuc_count, kernel_count), :] = dilated_ref[...]
    par_send[pl.ds(nuc_count + kernel_count, kernel_count), :] = short_ref[...]
    tok_send[...] = tok_ref[...].astype(jnp.float32).astype(jnp.bfloat16)
    load_filt.wait()
    largest = jnp.maximum(jnp.max(jnp.abs(filt_in[...]), axis=0, keepdims=True), LEAST)
    filt_size[...] = largest
    steps = steps_for(largest)
    for r in range(parts):
        turned[pl.ds(r, width, stride=parts), :] = (filt_in[pl.ds(r * LANES, LANES), :] * steps).T
    filt_send[...] = fixed_point(turned[...].reshape(filt_send.shape))
    load_cot.wait()
    for r in range(parts):
        turned[pl.ds(r, width, stride=parts), :] = cot_in[pl.ds(r * LANES, LANES), :].astype(jnp.float32).T
    cot_send[...] = turned[...].reshape(cot_send.shape).astype(jnp.bfloat16)
    await_all()

    params = pltpu.make_async_remote_copy(
        src_ref=par_send, dst_ref=par_all.at[place.side], send_sem=send_sem.at[0], recv_sem=recv_sem.at[0],
        device_id=place.device(1 - place.side, place.s), device_id_type=MESH)
    params.start()
    own_params = pltpu.make_async_copy(par_send, par_all.at[place.side], load_sem.at[2])
    own_params.start()

    def send_tokens(step, carry):
        pltpu.make_async_remote_copy(
            src_ref=tok_send, dst_ref=tok_all.at[place.s], send_sem=send_sem.at[1], recv_sem=recv_sem.at[1],
            device_id=place.device(place.side, place.near(step)), device_id_type=MESH).start()
        return carry

    lax.fori_loop(1, seq_count, send_tokens, 0)
    pltpu.make_async_copy(tok_send, tok_all.at[place.s], recv_sem.at[1]).start()

    def send(side, step):
        s = place.near(step)
        member = side * seq_count + s
        chunk = place.chunk_of(member, place.side)
        device = place.device(side, s)
        pltpu.make_async_remote_copy(
            src_ref=filt_send.at[chunk], dst_ref=filt_all.at[place.g], send_sem=send_sem.at[3],
            recv_sem=recv_sem.at[3], device_id=device, device_id_type=MESH).start()
        pltpu.make_async_remote_copy(
            src_ref=cot_send.at[chunk], dst_ref=cot_all.at[place.g], send_sem=send_sem.at[2],
            recv_sem=recv_sem.at[2], device_id=device, device_id_type=MESH).start()
        pltpu.make_async_remote_copy(
            src_ref=filt_size, dst_ref=filt_size_all.at[place.g], send_sem=send_sem.at[6],
            recv_sem=recv_sem.at[6], device_id=device, device_id_type=MESH).start()

    def send_four(index, carry):
        step = seq_count // 2 - index
        for far_step in (step, seq_count - step):
            send(place.side, far_step)
            send(1 - place.side, far_step)
        return carry

    send(place.side, seq_count // 2)
    send(1 - place.side, seq_count // 2)
    lax.fori_loop(1, seq_count // 2, send_four, 0)
    send(1 - place.side, 0)
    own = place.chunk_of(place.g, place.side)
    pltpu.make_async_copy(cot_send.at[own], cot_all.at[place.g], recv_sem.at[2]).start()
    pltpu.make_async_copy(filt_send.at[own], filt_all.at[place.g], recv_sem.at[3]).start()
    pltpu.make_async_copy(filt_size, filt_size_all.at[place.g], recv_sem.at[6]).start()

    for table in tables:
        table.wait()
    own_params.wait()
    params.wait()
    await_bytes(tok_all, recv_sem.at[1])

    flat = (seq_count * TILE, LANES)
    tiles = (seq_count, TILE, LANES)
    lane = lax.broadcasted_iota(jnp.int32, (1, TILE, LANES), 2)
    row = lax.broadcasted_iota(jnp.int32, (1, TILE, LANES), 1)
    width = par_all.shape[2]
    par_lane = lax.broadcasted_iota(jnp.int32, (TILE, width), 1)
    par_row = lax.broadcasted_iota(jnp.int32, (TILE, width), 0)
    tokens = tok_all[...].astype(jnp.float32)
    tokens = jnp.concatenate([tokens, tokens], axis=1)
    turn_re, turn_im = twiddle_ref[0], twiddle_ref[1]

    values, chosen = [], []
    for side in range(2):
        chunk = place.g if side == 0 else members - 1 - place.g
        here = par_lane == 2 * chunk + par_row // parts
        chosen.append(here[None])
        values.append([
            jnp.sum(jnp.where(here, par_all[side, pl.ds(k, 1), :], 0.0), axis=1, keepdims=True)[None]
            for k in range(nuc_count + 2 * kernel_count)
        ])
    for side in range(2):
        hidden = jnp.zeros(tiles, jnp.float32)
        for letter in range(nuc_count):
            hidden = jnp.where(tokens == float(letter), values[side][letter], hidden)
        hidden_ref[side] = hidden

    def fir(side, tap_side, sign):
        taps = values[tap_side][nuc_count:]
        if tap_side != side:
            taps = [jnp.where(row < parts, t[:, TILE - 1:, :], t[:, :1, :]) for t in taps]
        source = hidden_ref[side]
        inner = taps[0] * source
        for k in range(1, kernel_count):
            inner = inner + taps[k] * shifted(source, sign * k * SHORT_DILATION, lane, row, parts)
        taps = taps[kernel_count:]
        conv = taps[0] * inner
        for k in range(1, kernel_count):
            conv = conv + taps[k] * shifted(inner, sign * k, lane, row, parts)
        return conv.reshape(flat)

    def transform(pair, slots):
        both = jnp.concatenate(pair, axis=1)
        section = dot_left(first_ref, both)
        stack = []
        for index in range(2):
            cols = slice(index * LANES, (index + 1) * LANES)
            for jj in range(2):
                re = section[2 * jj * rows:(2 * jj + 1) * rows, cols]
                im = section[(2 * jj + 1) * rows:(2 * jj + 2) * rows, cols]
                stack.append(jnp.concatenate([re * turn_re - im * turn_im, re * turn_im + im * turn_re], axis=1))
        spec = dot_right(jnp.concatenate(stack, axis=0), second_ref)
        for index in range(2):
            for jj in range(2):
                at = (index * 2 + jj) * rows
                spec_ref[slots[index] + jj] = spec[at:at + rows]

    for side in range(2):
        transform([fir(side, side, 1), fir(side, 1 - side, -1)], (8 * side, 8 * side + 2))
    await_bytes(cot_all, recv_sem.at[2])
    await_bytes(filt_all, recv_sem.at[3])
    await_bytes(filt_size_all, recv_sem.at[6])
    for side in range(2):
        block = slice(side * seq_count, (side + 1) * seq_count)
        seed = cot_all[block].astype(jnp.float32) * hidden_ref[side]
        size = jnp.sum(jnp.where(chosen[side], filt_size_all[block], 0.0), axis=2, keepdims=True)
        filt = floating(filt_all[block]) * (size * (1.0 / COUNTS))
        transform([filt.reshape(flat), seed.reshape(flat)], (8 * side + 4, 8 * side + 6))

    def parts_of(side, kind, jj):
        full = spec_ref[8 * side + 2 * kind + jj]
        return full[:, :LANES], full[:, LANES:]

    def times(a, b):
        return a[0] * b[0] - a[1] * b[1], a[0] * b[1] + a[1] * b[0]

    def times_conj(a, b):
        return a[0] * b[0] + a[1] * b[1], a[1] * b[0] - a[0] * b[1]

    for side in range(2):
        stack = []
        for jj in range(2):
            other = (1 - side, 1 - jj)
            u, v, h, s = [parts_of(side, kind, jj) for kind in range(4)]
            v_far, h_far, s_far = [parts_of(other[0], kind, other[1]) for kind in range(1, 4)]
            long_spec = [x + y for x, y in zip(times(h, u), times_conj(v, h_far))]
            grad_spec = [x + y for x, y in zip(times_conj(s, u), times_conj(v_far, s_far))]
            stack.append(jnp.concatenate(long_spec, axis=1))
            stack.append(jnp.concatenate(grad_spec, axis=1))
        section = dot_right(jnp.concatenate(stack, axis=0), second_back_ref)
        columns = []
        for index in range(2):
            pieces = []
            for jj in range(2):
                at = (2 * jj + index) * rows
                re, im = section[at:at + rows, :LANES], section[at:at + rows, LANES:]
                pieces.append(re * turn_re + im * turn_im)
                pieces.append(im * turn_re - re * turn_im)
            columns.append(jnp.concatenate(pieces, axis=0))
        wave = dot_left(first_back_ref, jnp.concatenate(columns, axis=1))
        block = slice(side * seq_count, (side + 1) * seq_count)
        mixed_ref[block] = (hidden_ref[side] * wave[:, :LANES].reshape(tiles)).astype(jnp.bfloat16)
        grad = wave[:, LANES:].reshape(tiles)
        largest = [
            jnp.maximum(jnp.max(jnp.where(row // parts == jj, jnp.abs(grad), 0.0), axis=(1, 2), keepdims=True), LEAST)
            for jj in range(2)
        ]
        grad_size[block] = jnp.where(lane[:, :1] < LANES // 2, largest[0], largest[1])
        grad_ref[block] = fixed_point(grad * jnp.where(row < parts, steps_for(largest[0]), steps_for(largest[1])))

        def give_back(step, carry):
            s = place.near(step)
            device = place.device(side, s)
            member = side * seq_count + s
            chunk = place.chunk_of(place.g, side)
            pltpu.make_async_remote_copy(
                src_ref=grad_ref.at[member], dst_ref=grad_all.at[chunk], send_sem=send_sem.at[5],
                recv_sem=recv_sem.at[5], device_id=device, device_id_type=MESH).start()
            pltpu.make_async_remote_copy(
                src_ref=mixed_ref.at[member], dst_ref=mixed_all.at[chunk], send_sem=send_sem.at[4],
                recv_sem=recv_sem.at[4], device_id=device, device_id_type=MESH).start()
            pltpu.make_async_remote_copy(
                src_ref=grad_size.at[member], dst_ref=grad_size_all.at[chunk], send_sem=send_sem.at[7],
                recv_sem=recv_sem.at[7], device_id=device, device_id_type=MESH).start()
            return carry

        def give_pair(index, carry):
            step = seq_count // 2 - index
            give_back(step, carry)
            return give_back(seq_count - step, carry)

        give_back(seq_count // 2, 0)
        lax.fori_loop(1, seq_count // 2, give_pair, 0)

        @pl.when(place.side == side)
        def _():
            pltpu.make_async_copy(mixed_ref.at[place.g], mixed_all.at[own], recv_sem.at[4]).start()
            pltpu.make_async_copy(grad_ref.at[place.g], grad_all.at[own], recv_sem.at[5]).start()
            pltpu.make_async_copy(grad_size.at[place.g], grad_size_all.at[own], recv_sem.at[7]).start()

        @pl.when(place.side != side)
        def _():
            give_back(0, 0)

    await_bytes(tok_all.at[pl.ds(0, seq_count - 1)], send_sem.at[1])
    await_bytes(cot_send.at[pl.ds(0, members - 1)], send_sem.at[2])
    await_bytes(filt_send.at[pl.ds(0, members - 1)], send_sem.at[3])
    await_bytes(filt_size_all.at[pl.ds(0, members - 1)], send_sem.at[6])
    await_bytes(mixed_ref.at[pl.ds(0, members - 1)], send_sem.at[4])
    await_bytes(grad_ref.at[pl.ds(0, members - 1)], send_sem.at[5])
    await_bytes(grad_size.at[pl.ds(0, members - 1)], send_sem.at[7])
    await_bytes(mixed_all, recv_sem.at[4])
    await_bytes(grad_all, recv_sem.at[5])
    await_bytes(grad_size_all, recv_sem.at[7])


def settle_kernel(mixed_hbm, grad_hbm, size_hbm, mixed_out, grad_out, mixed_all, grad_all, size_all, turned, mixed_ref, grad_ref,
                  load_sem, store_sem):
    parts = grad_ref.shape[0] // LANES
    width = grad_ref.shape[1]
    loads = [
        pltpu.make_async_copy(far, near, load_sem.at[index])
        for index, (far, near) in enumerate([(mixed_hbm, mixed_all), (grad_hbm, grad_all), (size_hbm, size_all)])
    ]
    for load in loads:
        load.start()
    row = lax.broadcasted_iota(jnp.int32, (1, TILE, LANES), 1)
    stores = []

    def turn(values, into, out, sem):
        turned[...] = values.reshape(turned.shape)
        for r in range(parts):
            into[pl.ds(r * LANES, LANES), :] = turned[pl.ds(r, width, stride=parts), :].T.astype(into.dtype)
        stores.append(pltpu.make_async_copy(into, out, sem))
        stores[-1].start()

    loads[0].wait()
    turn(mixed_all[...].astype(jnp.float32), mixed_ref, mixed_out, store_sem.at[0])
    loads[1].wait()
    loads[2].wait()
    size = size_all[...] * (1.0 / COUNTS)
    size = jnp.where(row < parts, size[:, :, :1], size[:, :, LANES - 1:])
    turn(floating(grad_all[...]) * size, grad_ref, grad_out, store_sem.at[1])
    for store in stores:
        store.wait()


def local(seq_count, ch_count, tokens, embedding, taps_dilated, taps_short, long_filter, cotangent):
    block_rows, width = cotangent.shape
    kernel_count = taps_dilated.shape[0]
    nuc_count = embedding.shape[0]
    parts = block_rows // LANES
    members = 2 * seq_count
    rows = parts * seq_count
    assert 2 * parts == TILE and width == 2 * members
    vmem = pl.BlockSpec(memory_space=pltpu.VMEM)
    f32, bf16, i16 = jnp.float32, jnp.bfloat16, jnp.int16
    shape = jax.ShapeDtypeStruct
    limit = 67043328

    far = pl.BlockSpec(memory_space=pltpu.HBM)
    tables = [jnp.asarray(t) for t in dft_tables(seq_count, parts)]
    returned = pl.pallas_call(
        functools.partial(whole_kernel, seq_count, ch_count),
        out_shape=(
            shape((members, TILE, LANES), bf16),
            shape((members, TILE, LANES), i16),
            shape((members, 1, LANES), f32),
        ),
        in_specs=[far] * 11,
        out_specs=(far,) * 3,
        scratch_shapes=[
            pltpu.VMEM((parts, LANES), jnp.int32),
            pltpu.VMEM(embedding.shape, bf16),
            pltpu.VMEM(taps_dilated.shape, f32),
            pltpu.VMEM(taps_short.shape, f32),
            pltpu.VMEM((block_rows, width), bf16),
            pltpu.VMEM((block_rows, width), f32),
            pltpu.VMEM((members * TILE, LANES), f32),
            pltpu.VMEM((parts, LANES), bf16),
            pltpu.VMEM((-(-(nuc_count + 2 * kernel_count) // TILE) * TILE, width), f32),
            pltpu.VMEM((members, TILE, LANES), bf16),
            pltpu.VMEM((members, TILE, LANES), i16),
            pltpu.VMEM((1, width), f32),
            pltpu.VMEM((seq_count, parts, LANES), bf16),
            pltpu.VMEM((2, -(-(nuc_count + 2 * kernel_count) // TILE) * TILE, width), f32),
            pltpu.VMEM((members, TILE, LANES), bf16),
            pltpu.VMEM((members, TILE, LANES), i16),
            pltpu.VMEM((members, 1, width), f32),
            *[pltpu.VMEM(t.shape, t.dtype) for t in tables],
            pltpu.VMEM((2, seq_count, TILE, LANES), f32),
            pltpu.VMEM((16, rows, 2 * LANES), f32),
            pltpu.VMEM((members, TILE, LANES), bf16),
            pltpu.VMEM((members, TILE, LANES), i16),
            pltpu.VMEM((members, 1, LANES), f32),
            pltpu.SemaphoreType.DMA((4,)),
            pltpu.SemaphoreType.DMA((3,)),
            pltpu.SemaphoreType.DMA((5,)),
            pltpu.SemaphoreType.DMA((8,)),
            pltpu.SemaphoreType.DMA((8,)),
        ],
        compiler_params=pltpu.CompilerParams(collective_id=0, has_side_effects=True, vmem_limit_bytes=limit),
        name="whole",
    )(tokens.reshape(parts, LANES), embedding, taps_dilated, taps_short, cotangent, long_filter, *tables)

    return pl.pallas_call(
        settle_kernel,
        out_shape=(shape((block_rows, width), bf16), shape((block_rows, width), f32)),
        in_specs=[far] * 3,
        out_specs=(far,) * 2,
        scratch_shapes=[
            pltpu.VMEM((members, TILE, LANES), bf16),
            pltpu.VMEM((members, TILE, LANES), i16),
            pltpu.VMEM((members, 1, LANES), f32),
            pltpu.VMEM((members * TILE, LANES), f32),
            pltpu.VMEM((block_rows, width), bf16),
            pltpu.VMEM((block_rows, width), f32),
            pltpu.SemaphoreType.DMA((3,)),
            pltpu.SemaphoreType.DMA((2,)),
        ],
        compiler_params=pltpu.CompilerParams(vmem_limit_bytes=limit),
        name="settle",
    )(*returned)


def solution(mesh):
    in_specs = (
        P("seq"),
        P(None, "ch"),
        P(None, "ch"),
        P(None, "ch"),
        P("seq", "ch"),
        P("seq", "ch"),
    )
    out_specs = (P("seq", "ch"), P("seq", "ch"))
    body = functools.partial(local, mesh.shape["seq"], mesh.shape["ch"])
    return jax.shard_map(body, mesh=mesh, in_specs=in_specs, out_specs=out_specs, check_vma=False)
```
